32 devices in a mesh: dp: 8 (over z, core), seq: 4 (over y, x).
Axes of the slice: x: 2, y: 2, z: 4, core: 2. Of those that a mesh axis runs over, the one named last changes fastest.
Arguments:
- normed_tokens: bfloat16 [8, 512, 5120], P('dp', 'seq'), may hold values from -6 to 6
- query_by_head: bfloat16 [8, 512, 3072], P('dp', None, 'seq'), may hold values from -6 to 6
- key_by_head: bfloat16 [8, 512, 3072], P('dp', None, 'seq'), may hold values from -6 to 6
- value_by_head: bfloat16 [8, 512, 3072], P('dp', None, 'seq'), may hold values from -6 to 6
- output_gradient: bfloat16 [8, 512, 3072], P('dp', 'seq'), may hold values from -6 to 6
- delta_by_head: float32 [8, 512, 24], P('dp', None, 'seq'), may hold values from -15 to 15
- outer_log_mass: float32 [8, 512, 24], P('dp', None, 'seq'), may hold values from 2 to 10
- adapter_down_factors: bfloat16 [5120, 24], replicated, may hold values from -0.078125 to 0.078125
- adapter_up_factors: bfloat16 [24, 3072], replicated, may hold values from -1.75 to 1.75
- float_params: float32 [1536, 128], P(('dp', 'seq')), may hold values from -1.2 to 1.2
- first_moments: float32 [1536, 128], P(('dp', 'seq')), may hold values from -12 to 12
- second_moments: float32 [1536, 128], P(('dp', 'seq')), may hold values from 1 to 400
- average_params: float32 [1536, 128], P(('dp', 'seq')), may hold values from -1.2 to 1.2
Outputs:
- master_new: float32 [1536, 128], P(('dp', 'seq'))
- first_new: float32 [1536, 128], P(('dp', 'seq'))
- second_new: float32 [1536, 128], P(('dp', 'seq'))
- ema_new: float32 [1536, 128], P(('dp', 'seq'))
The draws below stay inside these ranges and needn't reach their ends.
All inputs are finite; a program needn't handle non-finite values.
Results may differ from the reference program's by a relative error of at most 0.013.
Values may be sent and summed in bfloat16 or wider, within the bound.
A program may use at most 64 MiB of HBM per device.

```python
import math
import jax
import jax.numpy as jnp
from jax import lax

MODEL_WIDTH = 5120
HEAD_SIZE = 128
HEAD_COUNT = 24
ADAPTER_RANK = 12
SEQLEN = 512
BATCH = 8
PARAM_ROWS = 1536


def drawn_pair(key):
    base_key = jax.random.fold_in(key, 101)
    key_list = jax.random.split(base_key, 2)
    feature_width = HEAD_COUNT * HEAD_SIZE
    shape_full = (BATCH, SEQLEN, feature_width)
    queries = jnp.clip(jax.random.normal(key_list[0], shape_full, jnp.float32), -6.0, 6.0)
    keyset = jnp.clip(jax.random.normal(key_list[1], shape_full, jnp.float32), -6.0, 6.0)
    return (queries, keyset)


def draw_query_by_head(key, part):
    return drawn_pair(key)[0].astype(jnp.bfloat16)


def draw_key_by_head(key, part):
    return drawn_pair(key)[1].astype(jnp.bfloat16)


def raised(values, rng, source, target, blocks, factor):
    owner, partner = [(jnp.arange(values.shape[axis_at]) // (values.shape[axis_at] // blocks)).reshape([-1 if axis == axis_at else 1 for axis in range(values.ndim)]) for axis_at in (source, target)]
    chosen = jax.random.permutation(rng, blocks)[partner]
    strong = (owner == chosen) | (owner == (partner + blocks // 2) % blocks)
    return jnp.where(strong, factor * values, values)


def block_levels(key, extent, pieces, low, largest):
    gain, own = 1.0, jax.random.fold_in(key, 6)
    for axis_at, parts in pieces:
        heights = jnp.exp(jax.random.uniform(jax.random.fold_in(own, axis_at), (parts,), jnp.float32, low / len(pieces), largest / len(pieces)))
        gain = gain * jnp.repeat(heights, extent[axis_at] // parts).reshape([-1 if axis == axis_at else 1 for axis in range(len(extent))])
    return gain


def bell_draw(own_key, dims, spread, bound, shards=(), kind=jnp.bfloat16):
    loudness = block_levels(own_key, dims, shards, -0.22, 0.18) if shards else 1.0
    entries = jax.random.normal(own_key, dims, jnp.float32) * spread * loudness
    return jnp.minimum(jnp.maximum(entries, -bound), bound).astype(kind)


def gaussian_with(rng, dims, spread, limit, pieces, heavy, held_as=jnp.bfloat16):
    entries = spread * jax.random.normal(rng, dims, jnp.float32)
    if pieces:
        entries = entries * block_levels(rng, dims, pieces, -0.22, 0.18)
    return jnp.clip(raised(entries, jax.random.fold_in(rng, 3), *heavy), -limit, limit).astype(held_as)


def setup_inputs(seed: int = 0) -> dict:
    keys = jax.random.split(jax.random.key(seed), 14)
    return {
        "normed_tokens": gaussian_with(keys[0], (BATCH, SEQLEN, MODEL_WIDTH), 1.0, 6.0, ((0, 8), (1, 4)), (0, 2, 8, 2.0)),
        "query_by_head": draw_query_by_head(jax.random.fold_in(keys[13], 71), 0),
        "key_by_head": draw_key_by_head(jax.random.fold_in(keys[13], 71), 0),
        "value_by_head": bell_draw(keys[3], (BATCH, SEQLEN, HEAD_COUNT * HEAD_SIZE), 1.0, 6.0, ((0, 8), (2, 4))),
        "output_gradient": gaussian_with(keys[4], (BATCH, SEQLEN, HEAD_COUNT * HEAD_SIZE), 1.0, 6.0, ((0, 8), (1, 4)), (0, 2, 8, 2.0)),
        "delta_by_head": bell_draw(keys[5], (BATCH, SEQLEN, HEAD_COUNT), 3.0, 15.0, ((0, 8), (2, 4)), jnp.float32),
        "outer_log_mass": jnp.clip(2.0 + 8.0 * jax.random.uniform(keys[6], (BATCH, SEQLEN, HEAD_COUNT), jnp.float32) ** block_levels(keys[6], (BATCH, SEQLEN, HEAD_COUNT), ((0, 8), (2, 4)), -0.2, 0.2), 2.0, 10.0),
        "adapter_down_factors": bell_draw(keys[7], (MODEL_WIDTH, 2 * ADAPTER_RANK), MODEL_WIDTH ** -0.5, 0.078125),
        "adapter_up_factors": bell_draw(keys[8], (2 * ADAPTER_RANK, HEAD_COUNT * HEAD_SIZE), ADAPTER_RANK ** -0.5, 1.75),
        "float_params": bell_draw(keys[9], (PARAM_ROWS, 128), 0.2, 1.2, ((0, 32),), jnp.float32),
        "first_moments": bell_draw(keys[10], (PARAM_ROWS, 128), 2.0, 12.0, ((0, 32),), jnp.float32),
        "second_moments": jnp.clip(jnp.exp(math.log(400.0) - 5.9914645 * jax.random.uniform(keys[11], (PARAM_ROWS, 128), jnp.float32) ** block_levels(keys[11], (PARAM_ROWS, 128), ((0, 32),), -0.2, 0.2)), 1.0, 400.0),
        "average_params": bell_draw(keys[12], (PARAM_ROWS, 128), 0.2, 1.2, ((0, 32),), jnp.float32),
    }


beta_first = 0.9
beta_second = 0.95
learn_rate = 0.02
decay_weight = 0.1
ema_decay = 0.999
adam_epsilon = 1e-08
adapter_factor = 2.0

def contract_dims(first_op, second_op, first_dim, second_dim):
    return lax.dot_general(first_op, second_op, (((first_dim,), (second_dim,)), ((), ())), preferred_element_type=jnp.float32)

def attend_back(query_rows, key_rows, value_rows, grad_rows, delta_row, outside_row):
    factor = query_rows.shape[-1] ** (-0.5)
    score = contract_dims(query_rows, key_rows, 1, 1) * factor
    outside_col = outside_row[:, None]
    top_score = jnp.maximum(lax.optimization_barrier(jnp.max(score, axis=1, keepdims=True)), outside_col)
    expo = jnp.exp(score - top_score)
    denom = lax.optimization_barrier(jnp.sum(expo, axis=1, keepdims=True)) + jnp.exp(outside_col - top_score)
    probs = expo / denom
    probs_low = probs.astype(jnp.bfloat16)
    grad_value = contract_dims(probs_low, grad_rows, 0, 0).astype(jnp.bfloat16)
    grad_prob = contract_dims(grad_rows, value_rows, 1, 1)
    grad_score = (probs * (grad_prob - delta_row[:, None])).astype(jnp.bfloat16)
    grad_query = (contract_dims(grad_score, key_rows, 1, 0) * factor).astype(jnp.bfloat16)
    return (grad_query, grad_value)

def adapter_terms(input_arrays, gradient_list, adapter_down_factors, adapter_up_factors):
    adapter_width = adapter_up_factors.shape[0] // 2
    projected_rows = jnp.dot(input_arrays, adapter_down_factors, preferred_element_type=jnp.float32).astype(jnp.bfloat16)
    middle_rows = jnp.concatenate([contract_dims(gradient_list[adapter_pair], adapter_up_factors[adapter_pair * adapter_width:(adapter_pair + 1) * adapter_width], 1, 1) for adapter_pair in range(2)], axis=1).astype(jnp.bfloat16)
    down_gradient = adapter_factor * contract_dims(input_arrays, middle_rows, 0, 0)
    up_gradient = jnp.concatenate([adapter_factor * contract_dims(projected_rows[:, adapter_pair * adapter_width:(adapter_pair + 1) * adapter_width], gradient_list[adapter_pair], 0, 0) for adapter_pair in range(2)], axis=0)
    return (down_gradient, up_gradient)

def adam_update(grads, float_params, first_moments, second_moments, average_params):
    first_new = beta_first * first_moments + (1.0 - beta_first) * grads
    second_new = beta_second * second_moments + (1.0 - beta_second) * grads * grads
    master_new = float_params - learn_rate * (first_new / (jnp.sqrt(second_new) + adam_epsilon) + decay_weight * float_params)
    ema_new = ema_decay * average_params + (1.0 - ema_decay) * master_new
    return (master_new, first_new, second_new, ema_new)

def reference(normed_tokens, query_by_head, key_by_head, value_by_head, output_gradient, delta_by_head, outer_log_mass, adapter_down_factors, adapter_up_factors, float_params, first_moments, second_moments, average_params):

    def split_heads(array):
        return array.reshape(SEQLEN, HEAD_COUNT, HEAD_SIZE).transpose(1, 0, 2)

    def merge_heads(array):
        return array.transpose(1, 0, 2).reshape(SEQLEN, HEAD_COUNT * HEAD_SIZE)

    def per_sample(carry, items):
        draw_input, sample_query, sample_key, sample_value, sample_grad, sample_delta, sample_outside = items
        bundle_in = (split_heads(sample_query), split_heads(sample_key), split_heads(sample_value), split_heads(sample_grad), sample_delta.T, sample_outside.T)
        grad_query, grad_value = lax.map(lambda bundle: attend_back(*bundle), bundle_in)
        gradient_list = [merge_heads(grad_query), merge_heads(grad_value)]
        down_gradient, up_gradient = adapter_terms(draw_input, gradient_list, adapter_down_factors, adapter_up_factors)
        return ((carry[0] + down_gradient, carry[1] + up_gradient), None)
    start_carry = (jnp.zeros((MODEL_WIDTH, 2 * ADAPTER_RANK), jnp.float32), jnp.zeros((2 * ADAPTER_RANK, HEAD_COUNT * HEAD_SIZE), jnp.float32))
    totals, _ = lax.scan(per_sample, start_carry, (normed_tokens, query_by_head, key_by_head, value_by_head, output_gradient, delta_by_head, outer_log_mass))
    grads = jnp.concatenate([totals[0].reshape(-1), totals[1].reshape(-1)]).reshape(-1, 128)
    master_new, first_new, second_new, ema_new = adam_update(grads, float_params, first_moments, second_moments, average_params)
    return (master_new, first_new, second_new, ema_new)
```

```python
import functools
import math

import jax
import jax.numpy as jnp
from jax import lax
from jax.experimental import pallas as pl
from jax.experimental.pallas import tpu as pltpu
from jax.sharding import PartitionSpec as P

HEAD_SIZE = 128
LANES = 128
PAIR = 2
MESH = pl.DeviceIdType.MESH


beta_first = 0.9
beta_second = 0.95
learn_rate = 0.02
decay_weight = 0.1
ema_decay = 0.999
adam_epsilon = 1e-08
adapter_factor = 2.0


def for_sending(array):
    return jax.tree.map(lambda a: a.astype(jnp.bfloat16) if a.dtype == jnp.float32 else a, array)


def contract_dims(first_op, second_op, first_dim, second_dim):
    return lax.dot_general(
        first_op,
        second_op,
        (((first_dim,), (second_dim,)), ((), ())),
        preferred_element_type=jnp.float32,
    )


def attend_blocks(query_rows, key_rows, value_rows, grad_rows, delta_row, outside_row):
    factor = query_rows.shape[-1] ** (-0.5)
    length = query_rows.shape[0]
    block_rows = 512
    query_parts = []
    value_total = jnp.zeros(value_rows.shape, jnp.float32)
    for block_index in range(length // block_rows):
        rows = slice(block_index * block_rows, (block_index + 1) * block_rows)
        query_block = query_rows[rows]
        grad_block = grad_rows[rows]
        outside_col = outside_row[rows][:, None]
        score = contract_dims(query_block, key_rows, 1, 1) * factor
        top_score = jnp.maximum(jnp.max(score, axis=1, keepdims=True), outside_col)
        expo = jnp.exp(score - top_score)
        denom = jnp.sum(expo, axis=1, keepdims=True) + jnp.exp(outside_col - top_score)
        probs = expo / denom
        probs_low = probs.astype(jnp.bfloat16)
        value_total = value_total + contract_dims(probs_low, grad_block, 0, 0)
        grad_prob = contract_dims(grad_block, value_rows, 1, 1)
        grad_score = (probs * (grad_prob - delta_row[rows][:, None])).astype(jnp.bfloat16)
        query_parts.append(
            (contract_dims(grad_score, key_rows, 1, 0) * factor).astype(jnp.bfloat16)
        )
    grad_query = jnp.concatenate(query_parts, axis=0)
    grad_value = value_total.astype(jnp.bfloat16)
    return (grad_query, grad_value)


def adapter_terms(input_arrays, gradient_list, adapter_down_factors, adapter_up_factors):
    adapter_width = adapter_up_factors.shape[0] // 2
    projected_rows = jnp.dot(
        input_arrays, adapter_down_factors, preferred_element_type=jnp.float32
    ).astype(jnp.bfloat16)
    middle_rows = jnp.concatenate(
        [
            contract_dims(
                gradient_list[adapter_pair],
                adapter_up_factors[
                    adapter_pair * adapter_width : (adapter_pair + 1) * adapter_width
                ],
                1,
                1,
            )
            for adapter_pair in range(2)
        ],
        axis=1,
    ).astype(jnp.bfloat16)
    down_gradient = adapter_factor * contract_dims(input_arrays, middle_rows, 0, 0)
    up_gradient = jnp.concatenate(
        [
            adapter_factor
            * contract_dims(
                projected_rows[
                    :, adapter_pair * adapter_width : (adapter_pair + 1) * adapter_width
                ],
                gradient_list[adapter_pair],
                0,
                0,
            )
            for adapter_pair in range(2)
        ],
        axis=0,
    )
    return (down_gradient, up_gradient)


def adam_update(grads, float_params, first_moments, second_moments, average_params):
    first_new = beta_first * first_moments + (1.0 - beta_first) * grads
    second_new = beta_second * second_moments + (1.0 - beta_second) * grads * grads
    master_new = float_params - learn_rate * (
        first_new / (jnp.sqrt(second_new) + adam_epsilon) + decay_weight * float_params
    )
    ema_new = ema_decay * average_params + (1.0 - ema_decay) * master_new
    return (master_new, first_new, second_new, ema_new)


def plain_local(
    normed_tokens,
    query_by_head,
    key_by_head,
    value_by_head,
    output_gradient,
    delta_by_head,
    outer_log_mass,
    adapter_down_factors,
    adapter_up_factors,
    float_params,
    first_moments,
    second_moments,
    average_params,
):
    grad_heads = lax.all_to_all(output_gradient, "seq", split_axis=2, concat_axis=1, tiled=True)
    length = query_by_head.shape[1]
    local_count = query_by_head.shape[2] // HEAD_SIZE

    def split_local(array):
        return array[0].reshape(length, local_count, HEAD_SIZE).transpose(1, 0, 2)

    def merge_local(array):
        return array.transpose(1, 0, 2).reshape(length, local_count * HEAD_SIZE)[None]

    bundle_in = (
        split_local(query_by_head),
        split_local(key_by_head),
        split_local(value_by_head),
        split_local(grad_heads),
        delta_by_head[0].T,
        outer_log_mass[0].T,
    )
    query_stack, value_stack = lax.map(lambda bundle: attend_blocks(*bundle), bundle_in)
    local_query = merge_local(query_stack)
    local_value = merge_local(value_stack)
    token_queries, token_values = (
        lax.all_to_all(
            for_sending(local_query), "seq", split_axis=1, concat_axis=2, tiled=True
        ).astype(local_query.dtype),
        lax.all_to_all(
            for_sending(local_value), "seq", split_axis=1, concat_axis=2, tiled=True
        ).astype(local_value.dtype),
    )
    down_gradient, up_gradient = adapter_terms(
        normed_tokens[0],
        [token_queries[0], token_values[0]],
        adapter_down_factors,
        adapter_up_factors,
    )
    term_rows = jnp.concatenate([down_gradient.reshape(-1), up_gradient.reshape(-1)]).reshape(
        -1, 128
    )
    partial_rows = lax.psum_scatter(term_rows, "dp", scatter_dimension=0, tiled=True)
    grads = lax.psum_scatter(partial_rows, "seq", scatter_dimension=0, tiled=True)
    master_new, first_new, second_new, ema_new = adam_update(
        grads, float_params, first_moments, second_moments, average_params
    )
    return (master_new, first_new, second_new, ema_new)


def fused_kernel(
    sizes,
    x_hbm,
    q_hbm,
    k_hbm,
    v_hbm,
    g_hbm,
    delta_hbm,
    mass_hbm,
    down_hbm,
    up_hbm,
    grads_ref,
    x_ref,
    q_ref,
    k_ref,
    v_ref,
    g_ref,
    delta_rows,
    mass_rows,
    down_ref,
    up_ref,
    proj_ref,
    probs_ref,
    gq_ref,
    gv_ref,
    mid_acc,
    mid_send,
    mid_recv,
    up_acc,
    up_send,
    up_recv,
    up2_send,
    up2_recv,
    down_send,
    down_recv,
    down2_send,
    down2_recv,
    flat_ref,
    load_sem,
    g_send_sem,
    g_recv_sem,
    proj_send_sem,
    proj_recv_sem,
    mid_send_sem,
    mid_recv_sem,
    d1_send_sem,
    d1_recv_sem,
    u1_send_sem,
    u1_recv_sem,
    p2_send_sem,
    p2_recv_sem,
):
    n_seq, nz = sizes["n_seq"], sizes["nz"]
    places = PAIR * n_seq
    down_count, down_block, up_rows = sizes["down_count"], sizes["down_block"], sizes["up_rows"]
    rank2 = up_ref.shape[0]
    width = q_ref.shape[1]
    heads = width // HEAD_SIZE
    length = q_ref.shape[0]
    tokens = x_ref.shape[0]
    factor = HEAD_SIZE ** (-0.5)

    my_dp, me = lax.axis_index("dp"), lax.axis_index("seq")
    my_z, my_core = my_dp // PAIR, my_dp % PAIR
    my_place = my_core * n_seq + me

    def plane_device(place):
        return (my_z * PAIR + place // n_seq, place % n_seq)

    def line_device(z):
        return (z * PAIR + my_core, me)

    barrier = pltpu.get_barrier_semaphore()
    for place in range(places):

        @pl.when(place != my_place)
        def _():
            pl.semaphore_signal(barrier, inc=1, device_id=plane_device(place), device_id_type=MESH)

    for z in range(nz):

        @pl.when(z != my_z)
        def _():
            pl.semaphore_signal(barrier, inc=1, device_id=line_device(z), device_id_type=MESH)

    my_columns = pl.ds(pl.multiple_of(me * width, LANES), width)
    my_tokens = pl.ds(pl.multiple_of(me * tokens, LANES), tokens)
    loads = [
        pltpu.make_async_copy(source, target, load_sem.at[index])
        for index, (source, target) in enumerate(
            (
                (mass_hbm, mass_rows),
                (k_hbm.at[0], k_ref),
                (q_hbm.at[0], q_ref),
                (x_hbm.at[0], x_ref),
                (down_hbm, down_ref),
                (delta_hbm, delta_rows),
                (v_hbm.at[0], v_ref),
                (g_hbm.at[0, :, my_columns], g_ref.at[my_tokens, :]),
                (up_hbm.at[:, my_columns], up_ref),
            )
        )
    ]
    for load in loads:
        load.start()
    def g_copy(step, head):
        target = lax.rem(me + step, n_seq)
        source_columns = pl.ds(pl.multiple_of(target * width + head * HEAD_SIZE, LANES), HEAD_SIZE)
        return pltpu.make_async_remote_copy(
            src_ref=g_hbm.at[0, :, source_columns],
            dst_ref=g_ref.at[my_tokens, pl.ds(pl.multiple_of(head * HEAD_SIZE, LANES), HEAD_SIZE)],
            send_sem=g_send_sem.at[step, head],
            recv_sem=g_recv_sem.at[step, head],
            device_id=(my_dp, target),
            device_id_type=MESH,
        )

    def proj_copy(step):
        return pltpu.make_async_remote_copy(
            src_ref=proj_ref.at[me],
            dst_ref=proj_ref.at[me],
            send_sem=proj_send_sem.at[step],
            recv_sem=proj_recv_sem.at[step],
            device_id=(my_dp, lax.rem(me + step, n_seq)),
            device_id_type=MESH,
        )

    block = min(256, length)

    def columns_of(head):
        return pl.ds(pl.multiple_of(head * HEAD_SIZE, LANES), HEAD_SIZE)

    def forward(head, carry):
        columns = columns_of(head)
        keys = k_ref[:, columns]
        for start in range(0, length, block):
            score = contract_dims(keys, q_ref[start : start + block, columns], 1, 1) * factor
            outside = mass_rows[head, :, start : start + block]
            top = jnp.maximum(jnp.max(score, axis=0, keepdims=True), outside)
            expo = jnp.exp(score - top)
            denom = jnp.sum(expo, axis=0, keepdims=True) + jnp.exp(outside - top)
            probs_ref[head, :, start : start + block] = (expo * (1.0 / denom)).astype(jnp.bfloat16)
        return carry

    pl.semaphore_wait(barrier, places - 1 + nz - 1)
    for head in range(heads):
        for step in range(1, n_seq):
            g_copy(step, head).start()

    for load in loads[:3]:
        load.wait()
    lax.fori_loop(0, heads, forward, 0)
    for load in loads[3:]:
        load.wait()
    projected = contract_dims(down_ref[...], x_ref[...], 1, 1)
    proj_ref[me] = projected.astype(jnp.bfloat16).astype(jnp.float32)
    for step in range(1, n_seq):
        proj_copy(step).start()
    mid_acc[...] = jnp.zeros_like(mid_acc)

    def backward(head, carry):
        columns = columns_of(head)
        for step in range(1, n_seq):
            g_copy(step, head).wait_recv()
        keys_turned = jnp.transpose(k_ref[:, columns])
        values = v_ref[:, columns]
        up_head = up_ref[:, columns]
        mids_q = []
        for start in range(0, length, block):
            rows = slice(start, start + block)
            grad_prob = contract_dims(values, g_ref[rows, columns], 1, 1)
            probs = probs_ref[head, :, rows].astype(jnp.float32)
            grad_score = (probs * (grad_prob - delta_rows[head, :, rows])).astype(jnp.bfloat16)
            grad_q = (contract_dims(keys_turned, grad_score, 1, 0) * factor).astype(jnp.bfloat16)
            gq_ref[columns, rows] = grad_q
            mids_q.append(contract_dims(up_head, grad_q, 1, 0))
        grad_v = contract_dims(probs_ref[head], g_ref[:, columns], 1, 0).astype(jnp.bfloat16)
        gv_ref[:, columns] = grad_v
        mids_v = contract_dims(up_head, grad_v, 1, 1)
        mid_first = lax.broadcasted_iota(jnp.int32, (rank2, length), 0) < rank2 // 2
        mid_acc[...] += jnp.where(mid_first, jnp.concatenate(mids_q, axis=1), mids_v)
        return carry

    lax.fori_loop(0, heads, backward, 0)

    for s in range(n_seq):
        mid_send[s] = mid_acc[:, s * tokens : (s + 1) * tokens]

    def mid_copy(step):
        target = lax.rem(me + step, n_seq)
        return pltpu.make_async_remote_copy(
            src_ref=mid_send.at[target],
            dst_ref=mid_recv.at[me],
            send_sem=mid_send_sem.at[step],
            recv_sem=mid_recv_sem.at[step],
            device_id=(my_dp, target),
            device_id_type=MESH,
        )

    for step in range(1, n_seq):
        mid_copy(step).start()
    mid_recv[me] = mid_send[me]

    for step in range(1, n_seq):
        proj_copy(step).wait_recv()
    proj_all = jnp.concatenate([proj_ref[s] for s in range(n_seq)], axis=1).astype(jnp.bfloat16)
    up_q = contract_dims(proj_all, gq_ref[...], 1, 1)
    up_v = contract_dims(proj_all, gv_ref[...], 1, 0)
    up_first = lax.broadcasted_iota(jnp.int32, (rank2, width), 0) < rank2 // 2
    up_acc[...] = adapter_factor * jnp.where(up_first, up_q, up_v)

    def d1_copy(owner):
        place, z = owner % places, owner // places
        return pltpu.make_async_remote_copy(
            src_ref=down_send.at[owner],
            dst_ref=down_recv.at[z, my_place],
            send_sem=d1_send_sem.at[owner],
            recv_sem=d1_recv_sem.at[z, my_place],
            device_id=plane_device(place),
            device_id_type=MESH,
        )

    def u1_copy(owner):
        place, z = owner % places, owner // places
        return pltpu.make_async_remote_copy(
            src_ref=up_send.at[owner - down_count],
            dst_ref=up_recv.at[z, my_place],
            send_sem=u1_send_sem.at[owner - down_count],
            recv_sem=u1_recv_sem.at[z, my_place],
            device_id=plane_device(place),
            device_id_type=MESH,
        )

    owners = nz * places
    for owner in range(down_count, owners):
        index = owner - down_count
        piece = up_acc[index * up_rows : (index + 1) * up_rows, :]
        up_send[index] = piece

        @pl.when(owner % places != my_place)
        def _():
            u1_copy(owner).start()

        @pl.when(owner % places == my_place)
        def _():
            up_recv[owner // places, my_place] = piece

    for step in range(1, n_seq):
        mid_copy(step).wait_recv()
    mids = mid_recv[0]
    for s in range(1, n_seq):
        mids = mids + mid_recv[s]
    mids = mids.astype(jnp.bfloat16)

    for owner in range(down_count):
        piece = contract_dims(mids, x_ref[:, owner * down_block : (owner + 1) * down_block], 1, 0)
        piece = (adapter_factor * piece).astype(down_send.dtype)
        down_send[owner] = piece

        @pl.when(owner % places != my_place)
        def _():
            d1_copy(owner).start()

        @pl.when(owner % places == my_place)
        def _():
            down_recv[owner // places, my_place] = piece

    def p2_down(z):
        return pltpu.make_async_remote_copy(
            src_ref=down2_send.at[z],
            dst_ref=down2_recv.at[my_z],
            send_sem=p2_send_sem.at[z],
            recv_sem=p2_recv_sem.at[my_z],
            device_id=line_device(z),
            device_id_type=MESH,
        )

    def p2_up(z):
        return pltpu.make_async_remote_copy(
            src_ref=up2_send.at[z],
            dst_ref=up2_recv.at[my_z],
            send_sem=p2_send_sem.at[z],
            recv_sem=p2_recv_sem.at[my_z],
            device_id=line_device(z),
            device_id_type=MESH,
        )

    def arrived(buffer, semaphores, z):
        for place in range(places):

            @pl.when(place != my_place)
            def _():
                pltpu.make_async_remote_copy(
                    src_ref=buffer.at[z, place],
                    dst_ref=buffer.at[z, place],
                    send_sem=semaphores.at[z, place],
                    recv_sem=semaphores.at[z, place],
                    device_id=plane_device(place),
                    device_id_type=MESH,
                ).wait_recv()

    for z in range(nz):
        is_down = z * places + my_place < down_count

        @pl.when(jnp.logical_not(is_down))
        def _():
            arrived(up_recv, u1_recv_sem, z)
            for s in range(n_seq):
                total = up_recv[z, s]
                for core in range(1, PAIR):
                    total = total + up_recv[z, core * n_seq + s]
                up2_send[z, s] = total

            @pl.when(z != my_z)
            def _():
                p2_up(z).start()

            @pl.when(z == my_z)
            def _():
                up2_recv[my_z] = up2_send[z]

    for z in range(nz):
        if z * places >= down_count:
            continue
        is_down = z * places + my_place < down_count

        @pl.when(is_down)
        def _():
            arrived(down_recv, d1_recv_sem, z)
            total = down_recv[z, 0].astype(jnp.float32)
            for place in range(1, places):
                total = total + down_recv[z, place].astype(jnp.float32)
            total = total.astype(down2_send.dtype)
            down2_send[z] = total

            @pl.when(z != my_z)
            def _():
                p2_down(z).start()

            @pl.when(z == my_z)
            def _():
                down2_recv[my_z] = total

    own_down = my_z * places + my_place < down_count

    @pl.when(own_down)
    def _():
        for z in range(nz):

            @pl.when(z != my_z)
            def _():
                pltpu.make_async_remote_copy(
                    src_ref=down2_recv.at[z],
                    dst_ref=down2_recv.at[z],
                    send_sem=p2_send_sem.at[z],
                    recv_sem=p2_recv_sem.at[z],
                    device_id=line_device(z),
                    device_id_type=MESH,
                ).wait_recv()

        total = down2_recv[0].astype(jnp.float32)
        for z in range(1, nz):
            total = total + down2_recv[z].astype(jnp.float32)
        padding = jnp.zeros((LANES - rank2, down_block), jnp.float32)
        flat_ref[...] = jnp.transpose(jnp.concatenate([total, padding], axis=0))
        period = LANES // math.gcd(LANES, rank2)
        span = period * rank2 // LANES
        groups = down_block // period
        lane = lax.broadcasted_iota(jnp.int32, (groups, LANES), 1)
        out_rows = [jnp.zeros((groups, LANES), jnp.float32) for _ in range(span)]
        for index in range(period):
            row, offset = divmod(index * rank2, LANES)
            entry = flat_ref[pl.ds(index, groups, stride=period), :]
            if offset:
                entry = pltpu.roll(entry, offset, 1)
            if offset + rank2 > LANES:
                out_rows[row] = out_rows[row] + jnp.where(lane >= offset, entry, 0.0)
                out_rows[row + 1] = out_rows[row + 1] + jnp.where(lane < offset, entry, 0.0)
            else:
                out_rows[row] = out_rows[row] + entry
        for row in range(span):
            grads_ref[pl.ds(row, groups, stride=span), :] = out_rows[row]

    @pl.when(jnp.logical_not(own_down))
    def _():
        for z in range(nz):

            @pl.when(z != my_z)
            def _():
                pltpu.make_async_remote_copy(
                    src_ref=up2_recv.at[z],
                    dst_ref=up2_recv.at[z],
                    send_sem=p2_send_sem.at[z],
                    recv_sem=p2_recv_sem.at[z],
                    device_id=line_device(z),
                    device_id_type=MESH,
                ).wait_recv()

        for s in range(n_seq):
            total = up2_recv[0, s]
            for z in range(1, nz):
                total = total + up2_recv[z, s]
            for row in range(up_rows):
                for tile in range(heads):
                    target = (row * n_seq + s) * heads + tile
                    grads_ref[target : target + 1, :] = total[
                        row : row + 1, tile * HEAD_SIZE : (tile + 1) * HEAD_SIZE
                    ]

    for step in range(1, n_seq):
        for head in range(heads):
            g_copy(step, head).wait_send()
        proj_copy(step).wait_send()
        mid_copy(step).wait_send()
    for owner in range(owners):

        @pl.when(owner % places != my_place)
        def _():
            (d1_copy if owner < down_count else u1_copy)(owner).wait_send()

    for z in range(nz):

        @pl.when((z != my_z) & (z * places + my_place < down_count))
        def _():
            p2_down(z).wait_send()

        @pl.when((z != my_z) & (z * places + my_place >= down_count))
        def _():
            p2_up(z).wait_send()


def fused_local(sizes, *arrays):
    (tokens_in, query, key, value, out_grad, delta, mass, down, up) = arrays[:9]
    n_seq, nz = sizes["n_seq"], sizes["nz"]
    places = PAIR * n_seq
    down_count, down_block, up_rows = sizes["down_count"], sizes["down_block"], sizes["up_rows"]
    up_count = nz * places - down_count
    tokens, model = tokens_in.shape[1:]
    length, width = query.shape[1:]
    heads = width // HEAD_SIZE
    rank2 = up.shape[0]
    down_planes = -(-down_count // places)
    f32, bf16 = jnp.float32, jnp.bfloat16
    dma = pltpu.SemaphoreType.DMA
    grads = pl.pallas_call(
        functools.partial(fused_kernel, sizes),
        out_shape=jax.ShapeDtypeStruct(arrays[9].shape, f32),
        in_specs=[pl.BlockSpec(memory_space=pl.ANY)] * 9,
        out_specs=pl.BlockSpec(memory_space=pltpu.VMEM),
        scratch_shapes=[
            pltpu.VMEM((tokens, model), bf16),
            pltpu.VMEM((length, width), bf16),
            pltpu.VMEM((length, width), bf16),
            pltpu.VMEM((length, width), bf16),
            pltpu.VMEM((length, width), bf16),
            pltpu.VMEM((heads, 1, length), f32),
            pltpu.VMEM((heads, 1, length), f32),
            pltpu.VMEM((rank2, model), bf16),
            pltpu.VMEM((rank2, width), bf16),
            pltpu.VMEM((n_seq, rank2, tokens), f32),
            pltpu.VMEM((heads, length, length), bf16),
            pltpu.VMEM((width, length), bf16),
            pltpu.VMEM((length, width), bf16),
            pltpu.VMEM((rank2, length), f32),
            pltpu.VMEM((n_seq, rank2, tokens), f32),
            pltpu.VMEM((n_seq, rank2, tokens), f32),
            pltpu.VMEM((rank2, width), f32),
            pltpu.VMEM((up_count, up_rows, width), f32),
            pltpu.VMEM((nz, places, up_rows, width), f32),
            pltpu.VMEM((nz, n_seq, up_rows, width), f32),
            pltpu.VMEM((nz, n_seq, up_rows, width), f32),
            pltpu.VMEM((down_count, rank2, down_block), bf16),
            pltpu.VMEM((down_planes, places, rank2, down_block), bf16),
            pltpu.VMEM((down_planes, rank2, down_block), bf16),
            pltpu.VMEM((nz, rank2, down_block), bf16),
            pltpu.VMEM((down_block, LANES), f32),
            dma((9,)),
            dma((n_seq, heads)),
            dma((n_seq, heads)),
            dma((n_seq,)),
            dma((n_seq,)),
            dma((n_seq,)),
            dma((n_seq,)),
            dma((down_count,)),
            dma((down_planes, places)),
            dma((up_count,)),
            dma((nz, places)),
            dma((nz,)),
            dma((nz,)),
        ],
        compiler_params=pltpu.CompilerParams(
            collective_id=0, has_side_effects=True, vmem_limit_bytes=24 * 1024 * 1024
        ),
        name="fused",
    )(
        *[
            pltpu.with_memory_space_constraint(array, pltpu.HBM)
            for array in (tokens_in, query, key, value, out_grad)
            + (delta.transpose(2, 0, 1), mass.transpose(2, 0, 1), down.T, up)
        ]
    )
    return adam_update(grads, *arrays[9:])


def fused_sizes(mesh, shapes):
    n_dp, n_seq = mesh.shape["dp"], mesh.shape["seq"]
    down, up, rows = shapes
    count = rows[0] // (n_dp * n_seq) * rows[1]
    if n_dp % PAIR or count % down[1] or count % up[1]:
        return None
    block, up_rows = count // down[1], count // up[1]
    period = LANES // math.gcd(LANES, down[1])
    if down[0] % block or block % LANES or block % period or up[0] % up_rows:
        return None
    return {
        "n_seq": n_seq,
        "nz": n_dp // PAIR,
        "down_count": down[0] // block,
        "down_block": block,
        "up_rows": up_rows,
    }


def solution(mesh):
    def step(*arrays):
        sizes = fused_sizes(mesh, (arrays[7].shape, arrays[8].shape, arrays[9].shape))
        rows = P(("dp", "seq"), None)
        by_token, by_head = P("dp", "seq", None), P("dp", None, "seq")
        return jax.shard_map(
            plain_local if sizes is None else functools.partial(fused_local, sizes),
            mesh=mesh,
            in_specs=(by_token, by_head, by_head, by_head, by_token, by_head, by_head)
            + (P(), P(), rows, rows, rows, rows),
            out_specs=(rows, rows, rows, rows),
            check_vma=False,
        )(*arrays)

    return step
```

```python
import functools
import math

import jax
import jax.numpy as jnp
from jax import lax
from jax.experimental import pallas as pl
from jax.experimental.pallas import tpu as pltpu
from jax.sharding import PartitionSpec as P

HEAD_SIZE = 128
LANES = 128
PAIR = 2
GROUP = 2
MESH = pl.DeviceIdType.MESH


beta_first = 0.9
beta_second = 0.95
learn_rate = 0.02
decay_weight = 0.1
ema_decay = 0.999
adam_epsilon = 1e-08
adapter_factor = 2.0


def for_sending(array):
    return jax.tree.map(lambda a: a.astype(jnp.bfloat16) if a.dtype == jnp.float32 else a, array)


def contract_dims(first_op, second_op, first_dim, second_dim):
    return lax.dot_general(
        first_op,
        second_op,
        (((first_dim,), (second_dim,)), ((), ())),
        preferred_element_type=jnp.float32,
    )


def attend_blocks(query_rows, key_rows, value_rows, grad_rows, delta_row, outside_row):
    factor = query_rows.shape[-1] ** (-0.5)
    length = query_rows.shape[0]
    block_rows = 512
    query_parts = []
    value_total = jnp.zeros(value_rows.shape, jnp.float32)
    for block_index in range(length // block_rows):
        rows = slice(block_index * block_rows, (block_index + 1) * block_rows)
        query_block = query_rows[rows]
        grad_block = grad_rows[rows]
        outside_col = outside_row[rows][:, None]
        score = contract_dims(query_block, key_rows, 1, 1) * factor
        top_score = jnp.maximum(jnp.max(score, axis=1, keepdims=True), outside_col)
        expo = jnp.exp(score - top_score)
        denom = jnp.sum(expo, axis=1, keepdims=True) + jnp.exp(outside_col - top_score)
        probs = expo / denom
        probs_low = probs.astype(jnp.bfloat16)
        value_total = value_total + contract_dims(probs_low, grad_block, 0, 0)
        grad_prob = contract_dims(grad_block, value_rows, 1, 1)
        grad_score = (probs * (grad_prob - delta_row[rows][:, None])).astype(jnp.bfloat16)
        query_parts.append(
            (contract_dims(grad_score, key_rows, 1, 0) * factor).astype(jnp.bfloat16)
        )
    grad_query = jnp.concatenate(query_parts, axis=0)
    grad_value = value_total.astype(jnp.bfloat16)
    return (grad_query, grad_value)


def adapter_terms(input_arrays, gradient_list, adapter_down_factors, adapter_up_factors):
    adapter_width = adapter_up_factors.shape[0] // 2
    projected_rows = jnp.dot(
        input_arrays, adapter_down_factors, preferred_element_type=jnp.float32
    ).astype(jnp.bfloat16)
    middle_rows = jnp.concatenate(
        [
            contract_dims(
                gradient_list[adapter_pair],
                adapter_up_factors[
                    adapter_pair * adapter_width : (adapter_pair + 1) * adapter_width
                ],
                1,
                1,
            )
            for adapter_pair in range(2)
        ],
        axis=1,
    ).astype(jnp.bfloat16)
    down_gradient = adapter_factor * contract_dims(input_arrays, middle_rows, 0, 0)
    up_gradient = jnp.concatenate(
        [
            adapter_factor
            * contract_dims(
                projected_rows[
                    :, adapter_pair * adapter_width : (adapter_pair + 1) * adapter_width
                ],
                gradient_list[adapter_pair],
                0,
                0,
            )
            for adapter_pair in range(2)
        ],
        axis=0,
    )
    return (down_gradient, up_gradient)


def adam_update(grads, float_params, first_moments, second_moments, average_params):
    first_new = beta_first * first_moments + (1.0 - beta_first) * grads
    second_new = beta_second * second_moments + (1.0 - beta_second) * grads * grads
    master_new = float_params - learn_rate * (
        first_new / (jnp.sqrt(second_new) + adam_epsilon) + decay_weight * float_params
    )
    ema_new = ema_decay * average_params + (1.0 - ema_decay) * master_new
    return (master_new, first_new, second_new, ema_new)


def plain_local(
    normed_tokens,
    query_by_head,
    key_by_head,
    value_by_head,
    output_gradient,
    delta_by_head,
    outer_log_mass,
    adapter_down_factors,
    adapter_up_factors,
    float_params,
    first_moments,
    second_moments,
    average_params,
):
    grad_heads = lax.all_to_all(output_gradient, "seq", split_axis=2, concat_axis=1, tiled=True)
    length = query_by_head.shape[1]
    local_count = query_by_head.shape[2] // HEAD_SIZE

    def split_local(array):
        return array[0].reshape(length, local_count, HEAD_SIZE).transpose(1, 0, 2)

    def merge_local(array):
        return array.transpose(1, 0, 2).reshape(length, local_count * HEAD_SIZE)[None]

    bundle_in = (
        split_local(query_by_head),
        split_local(key_by_head),
        split_local(value_by_head),
        split_local(grad_heads),
        delta_by_head[0].T,
        outer_log_mass[0].T,
    )
    query_stack, value_stack = lax.map(lambda bundle: attend_blocks(*bundle), bundle_in)
    local_query = merge_local(query_stack)
    local_value = merge_local(value_stack)
    token_queries, token_values = (
        lax.all_to_all(
            for_sending(local_query), "seq", split_axis=1, concat_axis=2, tiled=True
        ).astype(local_query.dtype),
        lax.all_to_all(
            for_sending(local_value), "seq", split_axis=1, concat_axis=2, tiled=True
        ).astype(local_value.dtype),
    )
    down_gradient, up_gradient = adapter_terms(
        normed_tokens[0],
        [token_queries[0], token_values[0]],
        adapter_down_factors,
        adapter_up_factors,
    )
    term_rows = jnp.concatenate([down_gradient.reshape(-1), up_gradient.reshape(-1)]).reshape(
        -1, 128
    )
    partial_rows = lax.psum_scatter(term_rows, "dp", scatter_dimension=0, tiled=True)
    grads = lax.psum_scatter(partial_rows, "seq", scatter_dimension=0, tiled=True)
    master_new, first_new, second_new, ema_new = adam_update(
        grads, float_params, first_moments, second_moments, average_params
    )
    return (master_new, first_new, second_new, ema_new)


def fused_kernel(
    sizes,
    x_hbm,
    q_hbm,
    k_hbm,
    v_hbm,
    g_hbm,
    delta_hbm,
    mass_hbm,
    down_hbm,
    up_hbm,
    grads_ref,
    x_ref,
    q_ref,
    k_ref,
    v_ref,
    g_ref,
    delta_rows,
    mass_rows,
    down_ref,
    up_ref,
    proj_ref,
    probs_ref,
    gq_ref,
    gv_ref,
    mid_acc,
    mid_send,
    mid_recv,
    up_acc,
    up_send,
    up_recv,
    x_part,
    down_send,
    down_recv,
    flat_ref,
    load_sem,
    ready_sem,
    g_send_sem,
    g_recv_sem,
    x_send_sem,
    x_recv_sem,
    proj_send_sem,
    proj_recv_sem,
    mid_send_sem,
    mid_recv_sem,
    down_send_sem,
    down_recv_sem,
    up_send_sem,
    up_recv_sem,
):
    n_seq, nz = sizes["n_seq"], sizes["nz"]
    places = PAIR * n_seq
    down_count, down_block, up_rows = sizes["down_count"], sizes["down_block"], sizes["up_rows"]
    rank2 = up_ref.shape[0]
    width = q_ref.shape[1]
    heads = width // HEAD_SIZE
    length = q_ref.shape[0]
    tokens = x_ref.shape[0]
    factor = HEAD_SIZE ** (-0.5)

    my_dp, me = lax.axis_index("dp"), lax.axis_index("seq")
    my_z, my_core = my_dp // PAIR, my_dp % PAIR
    my_place = my_core * n_seq + me
    my_flat = my_dp * n_seq + me
    member, first_member = my_dp % GROUP, my_dp // GROUP * GROUP
    teams = nz * PAIR // GROUP
    owners = nz * places
    share = down_count // GROUP
    part = share * down_block

    def plane_device(place):
        return (my_z * PAIR + place // n_seq, place % n_seq)

    def line_device(z):
        return (z * PAIR + my_core, me)

    def flat_device(owner):
        return (owner // n_seq, owner % n_seq)

    barrier = pltpu.get_barrier_semaphore()

    def greet(device):
        pl.semaphore_signal(barrier, inc=1, device_id=device, device_id_type=MESH)

    for step in range(1, places):
        greet(plane_device(lax.rem(my_place + step, places)))
    for step in range(1, nz):
        greet(line_device(lax.rem(my_z + step, nz)))
    greeted = places - 1 + nz - 1
    for step in range(PAIR, GROUP, PAIR):
        for core in range(1, PAIR):
            other = first_member + lax.rem(member // PAIR * PAIR + step, GROUP) + lax.rem(my_core + core, PAIR)
            greet((other, me))
            greeted += 1

    my_columns = pl.ds(pl.multiple_of(me * width, LANES), width)
    my_tokens = pl.ds(pl.multiple_of(me * tokens, LANES), tokens)
    loads = [
        pltpu.make_async_copy(source, target, load_sem.at[index])
        for index, (source, target) in enumerate(
            (
                (mass_hbm, mass_rows),
                (k_hbm.at[0], k_ref),
                (q_hbm.at[0], q_ref),
                (x_hbm.at[0], x_ref),
                (down_hbm, down_ref),
                (delta_hbm, delta_rows),
                (v_hbm.at[0], v_ref),
                (g_hbm.at[0, :, my_columns], g_ref.at[my_tokens, :]),
                (up_hbm.at[:, my_columns], up_ref),
                (
                    x_hbm.at[0, :, pl.ds(pl.multiple_of(member * part, LANES), part)],
                    x_part.at[pl.ds(pl.multiple_of(member * tokens, LANES), tokens), :],
                ),
            )
        )
    ]
    for load in loads:
        load.start()
    def g_copy(step, head):
        target = lax.rem(me + step, n_seq)
        source_columns = pl.ds(pl.multiple_of(target * width + head * HEAD_SIZE, LANES), HEAD_SIZE)
        return pltpu.make_async_remote_copy(
            src_ref=g_hbm.at[0, :, source_columns],
            dst_ref=g_ref.at[my_tokens, pl.ds(pl.multiple_of(head * HEAD_SIZE, LANES), HEAD_SIZE)],
            send_sem=g_send_sem.at[step, head],
            recv_sem=g_recv_sem.at[step, head],
            device_id=(my_dp, target),
            device_id_type=MESH,
        )

    def x_copy(step):
        target = lax.rem(member + step, GROUP)
        return pltpu.make_async_remote_copy(
            src_ref=x_hbm.at[0, :, pl.ds(pl.multiple_of(target * part, LANES), part)],
            dst_ref=x_part.at[pl.ds(pl.multiple_of(member * tokens, LANES), tokens), :],
            send_sem=x_send_sem.at[step],
            recv_sem=x_recv_sem.at[step],
            device_id=(first_member + target, me),
            device_id_type=MESH,
        )

    def proj_copy(step):
        return pltpu.make_async_remote_copy(
            src_ref=proj_ref.at[me],
            dst_ref=proj_ref.at[me],
            send_sem=proj_send_sem.at[step],
            recv_sem=proj_recv_sem.at[step],
            device_id=(my_dp, lax.rem(me + step, n_seq)),
            device_id_type=MESH,
        )

    block = min(256, length)

    def columns_of(head):
        return pl.ds(pl.multiple_of(head * HEAD_SIZE, LANES), HEAD_SIZE)

    def forward(head, carry):
        columns = columns_of(head)
        keys = k_ref[:, columns]
        for start in range(0, length, block):
            score = contract_dims(keys, q_ref[start : start + block, columns], 1, 1) * factor
            outside = mass_rows[head, :, start : start + block]
            top = jnp.maximum(jnp.max(score, axis=0, keepdims=True), outside)
            expo = jnp.exp(score - top)
            denom = jnp.sum(expo, axis=0, keepdims=True) + jnp.exp(outside - top)
            probs_ref[head, :, start : start + block] = (expo * (1.0 / denom)).astype(jnp.bfloat16)
        return carry

    pl.semaphore_wait(barrier, greeted)
    for head in range(heads):
        for step in range(1, n_seq):
            g_copy(step, head).start()
    for step in range(1, GROUP):
        x_copy(step).start()
    for step in range(1, places):
        pl.semaphore_signal(
            ready_sem,
            inc=1,
            device_id=plane_device(lax.rem(my_place + step, places)),
            device_id_type=MESH,
        )

    for load in loads[:3]:
        load.wait()
    lax.fori_loop(0, heads, forward, 0)
    for load in loads[3:]:
        load.wait()
    projected = contract_dims(down_ref[...], x_ref[...], 1, 1)
    proj_ref[me] = projected.astype(jnp.bfloat16).astype(jnp.float32)
    for step in range(1, n_seq):
        proj_copy(step).start()
    mid_acc[...] = jnp.zeros_like(mid_acc)

    def backward(head, carry):
        columns = columns_of(head)
        for step in range(1, n_seq):
            g_copy(step, head).wait_recv()
        keys_turned = jnp.transpose(k_ref[:, columns])
        values = v_ref[:, columns]
        up_head = up_ref[:, columns]
        mids_q = []
        for start in range(0, length, block):
            rows = slice(start, start + block)
            grad_prob = contract_dims(values, g_ref[rows, columns], 1, 1)
            probs = probs_ref[head, :, rows].astype(jnp.float32)
            grad_score = (probs * (grad_prob - delta_rows[head, :, rows])).astype(jnp.bfloat16)
            grad_q = (contract_dims(keys_turned, grad_score, 1, 0) * factor).astype(jnp.bfloat16)
            gq_ref[columns, rows] = grad_q
            mids_q.append(contract_dims(up_head, grad_q, 1, 0))
        grad_v = contract_dims(probs_ref[head], g_ref[:, columns], 1, 0).astype(jnp.bfloat16)
        gv_ref[:, columns] = grad_v
        mids_v = contract_dims(up_head, grad_v, 1, 1)
        mid_first = lax.broadcasted_iota(jnp.int32, (rank2, length), 0) < rank2 // 2
        mid_acc[...] += jnp.where(mid_first, jnp.concatenate(mids_q, axis=1), mids_v)
        return carry

    lax.fori_loop(0, heads, backward, 0)

    for s in range(n_seq):
        mid_send[s] = mid_acc[:, s * tokens : (s + 1) * tokens].astype(mid_send.dtype)
    pl.semaphore_wait(ready_sem, places - 1)

    my_slot = member * n_seq + me
    slots = GROUP * n_seq

    def mid_copy(step):
        target = lax.rem(my_slot + step, slots)
        return pltpu.make_async_remote_copy(
            src_ref=mid_send.at[target % n_seq],
            dst_ref=mid_recv.at[my_slot],
            send_sem=mid_send_sem.at[step],
            recv_sem=mid_recv_sem.at[step],
            device_id=(first_member + target // n_seq, target % n_seq),
            device_id_type=MESH,
        )

    for step in range(1, slots):
        mid_copy(step).start()
    mid_recv[my_slot] = mid_send[me]

    for step in range(1, n_seq):
        proj_copy(step).wait_recv()
    proj_all = jnp.concatenate([proj_ref[s] for s in range(n_seq)], axis=1).astype(jnp.bfloat16)
    up_q = contract_dims(proj_all, gq_ref[...], 1, 1)
    up_v = contract_dims(proj_all, gv_ref[...], 1, 0)
    up_first = lax.broadcasted_iota(jnp.int32, (rank2, width), 0) < rank2 // 2
    up_acc[...] = adapter_factor * jnp.where(up_first, up_q, up_v)

    def up_copy(index):
        return pltpu.make_async_remote_copy(
            src_ref=up_send.at[index],
            dst_ref=up_recv.at[my_dp, me],
            send_sem=up_send_sem.at[index],
            recv_sem=up_recv_sem.at[my_dp, me],
            device_id=flat_device(down_count + index),
            device_id_type=MESH,
        )

    for index in range(owners - down_count):
        piece = up_acc[index * up_rows : (index + 1) * up_rows, :]
        up_send[index] = piece

        @pl.when(down_count + index != my_flat)
        def _():
            up_copy(index).start()

        @pl.when(down_count + index == my_flat)
        def _():
            up_recv[my_dp, me] = piece

    for step in range(1, slots):
        mid_copy(step).wait_recv()
    mids = []
    for m in range(GROUP):
        total = mid_recv[m * n_seq].astype(jnp.float32)
        for s in range(1, n_seq):
            total = total + mid_recv[m * n_seq + s].astype(jnp.float32)
        mids.append(total.astype(jnp.bfloat16))
    mids = jnp.concatenate(mids, axis=1)
    for step in range(1, GROUP):
        x_copy(step).wait_recv()

    my_source = my_dp // GROUP * n_seq + me

    def down_copy(index):
        return pltpu.make_async_remote_copy(
            src_ref=down_send.at[index],
            dst_ref=down_recv.at[my_source],
            send_sem=down_send_sem.at[index],
            recv_sem=down_recv_sem.at[my_source],
            device_id=flat_device(member * share + index),
            device_id_type=MESH,
        )

    for index in range(share):
        piece = contract_dims(mids, x_part[:, index * down_block : (index + 1) * down_block], 1, 0)
        piece = (adapter_factor * piece).astype(down_send.dtype)
        down_send[index] = piece

        @pl.when(member * share + index != my_flat)
        def _():
            down_copy(index).start()

        @pl.when(member * share + index == my_flat)
        def _():
            down_recv[my_source] = piece

    def arrived(buffer, semaphore):
        pltpu.make_async_remote_copy(
            src_ref=buffer,
            dst_ref=buffer,
            send_sem=semaphore,
            recv_sem=semaphore,
            device_id=plane_device(lax.rem(my_place + 1, places)),
            device_id_type=MESH,
        ).wait_recv()

    own_down = my_flat < down_count

    @pl.when(own_down)
    def _():
        from_me = my_flat // share == member
        for source in range(teams * n_seq):

            @pl.when(jnp.logical_not(from_me & (my_source == source)))
            def _():
                arrived(down_recv.at[source], down_recv_sem.at[source])

        total = down_recv[0].astype(jnp.float32)
        for source in range(1, teams * n_seq):
            total = total + down_recv[source].astype(jnp.float32)
        padding = jnp.zeros((LANES - rank2, down_block), jnp.float32)
        flat_ref[...] = jnp.transpose(jnp.concatenate([total, padding], axis=0))
        period = LANES // math.gcd(LANES, rank2)
        span = period * rank2 // LANES
        groups = down_block // period
        lane = lax.broadcasted_iota(jnp.int32, (groups, LANES), 1)
        out_rows = [jnp.zeros((groups, LANES), jnp.float32) for _ in range(span)]
        for index in range(period):
            row, offset = divmod(index * rank2, LANES)
            entry = flat_ref[pl.ds(index, groups, stride=period), :]
            if offset:
                entry = pltpu.roll(entry, offset, 1)
            if offset + rank2 > LANES:
                out_rows[row] = out_rows[row] + jnp.where(lane >= offset, entry, 0.0)
                out_rows[row + 1] = out_rows[row + 1] + jnp.where(lane < offset, entry, 0.0)
            else:
                out_rows[row] = out_rows[row] + entry
        for row in range(span):
            grads_ref[pl.ds(row, groups, stride=span), :] = out_rows[row]

    @pl.when(jnp.logical_not(own_down))
    def _():
        for dp in range(nz * PAIR):
            for s in range(n_seq):

                @pl.when(dp * n_seq + s != my_flat)
                def _():
                    arrived(up_recv.at[dp, s], up_recv_sem.at[dp, s])

        for s in range(n_seq):
            total = up_recv[0, s]
            for dp in range(1, nz * PAIR):
                total = total + up_recv[dp, s]
            for row in range(up_rows):
                for tile in range(heads):
                    target = (row * n_seq + s) * heads + tile
                    grads_ref[target : target + 1, :] = total[
                        row : row + 1, tile * HEAD_SIZE : (tile + 1) * HEAD_SIZE
                    ]

    for step in range(1, n_seq):
        for head in range(heads):
            g_copy(step, head).wait_send()
        proj_copy(step).wait_send()
    for step in range(1, GROUP):
        x_copy(step).wait_send()
    for step in range(1, slots):
        mid_copy(step).wait_send()
    for index in range(owners - down_count):

        @pl.when(down_count + index != my_flat)
        def _():
            up_copy(index).wait_send()

    for index in range(share):

        @pl.when(member * share + index != my_flat)
        def _():
            down_copy(index).wait_send()


def fused_local(sizes, *arrays):
    (tokens_in, query, key, value, out_grad, delta, mass, down, up) = arrays[:9]
    n_seq, nz = sizes["n_seq"], sizes["nz"]
    places = PAIR * n_seq
    down_count, down_block, up_rows = sizes["down_count"], sizes["down_block"], sizes["up_rows"]
    up_count = nz * places - down_count
    tokens, model = tokens_in.shape[1:]
    length, width = query.shape[1:]
    heads = width // HEAD_SIZE
    rank2 = up.shape[0]
    teams, slots = nz * PAIR // GROUP, GROUP * n_seq
    share = down_count // GROUP
    f32, bf16 = jnp.float32, jnp.bfloat16
    dma = pltpu.SemaphoreType.DMA
    grads = pl.pallas_call(
        functools.partial(fused_kernel, sizes),
        out_shape=jax.ShapeDtypeStruct(arrays[9].shape, f32),
        in_specs=[pl.BlockSpec(memory_space=pl.ANY)] * 9,
        out_specs=pl.BlockSpec(memory_space=pltpu.VMEM),
        scratch_shapes=[
            pltpu.VMEM((tokens, model), bf16),
            pltpu.VMEM((length, width), bf16),
            pltpu.VMEM((length, width), bf16),
            pltpu.VMEM((length, width), bf16),
            pltpu.VMEM((length, width), bf16),
            pltpu.VMEM((heads, 1, length), f32),
            pltpu.VMEM((heads, 1, length), f32),
            pltpu.VMEM((rank2, model), bf16),
            pltpu.VMEM((rank2, width), bf16),
            pltpu.VMEM((n_seq, rank2, tokens), f32),
            pltpu.VMEM((heads, length, length), bf16),
            pltpu.VMEM((width, length), bf16),
            pltpu.VMEM((length, width), bf16),
            pltpu.VMEM((rank2, length), f32),
            pltpu.VMEM((n_seq, rank2, tokens), bf16),
            pltpu.VMEM((slots, rank2, tokens), bf16),
            pltpu.VMEM((rank2, width), f32),
            pltpu.VMEM((up_count, up_rows, width), f32),
            pltpu.VMEM((nz * PAIR, n_seq, up_rows, width), f32),
            pltpu.VMEM((GROUP * tokens, share * down_block), bf16),
            pltpu.VMEM((share, rank2, down_block), bf16),
            pltpu.VMEM((teams * n_seq, rank2, down_block), bf16),
            pltpu.VMEM((down_block, LANES), f32),
            dma((10,)),
            pltpu.SemaphoreType.REGULAR,
            dma((n_seq, heads)),
            dma((n_seq, heads)),
            dma((GROUP,)),
            dma((GROUP,)),
            dma((n_seq,)),
            dma((n_seq,)),
            dma((slots,)),
            dma((slots,)),
            dma((share,)),
            dma((teams * n_seq,)),
            dma((up_count,)),
            dma((nz * PAIR, n_seq)),
        ],
        compiler_params=pltpu.CompilerParams(
            collective_id=0, has_side_effects=True, vmem_limit_bytes=24 * 1024 * 1024
        ),
        name="fused",
    )(
        *[
            pltpu.with_memory_space_constraint(array, pltpu.HBM)
            for array in (tokens_in, query, key, value, out_grad)
            + (delta.transpose(2, 0, 1), mass.transpose(2, 0, 1), down.T, up)
        ]
    )
    return adam_update(grads, *arrays[9:])


def fused_sizes(mesh, shapes):
    n_dp, n_seq = mesh.shape["dp"], mesh.shape["seq"]
    down, up, rows = shapes
    count = rows[0] // (n_dp * n_seq) * rows[1]
    if n_dp % PAIR or n_dp % GROUP or count % down[1] or count % up[1]:
        return None
    block, up_rows = count // down[1], count // up[1]
    period = LANES // math.gcd(LANES, down[1])
    if down[0] % (block * GROUP) or block % LANES or block % period or up[0] % up_rows:
        return None
    return {
        "n_seq": n_seq,
        "nz": n_dp // PAIR,
        "down_count": down[0] // block,
        "down_block": block,
        "up_rows": up_rows,
    }


def solution(mesh):
    def step(*arrays):
        sizes = fused_sizes(mesh, (arrays[7].shape, arrays[8].shape, arrays[9].shape))
        rows = P(("dp", "seq"), None)
        by_token, by_head = P("dp", "seq", None), P("dp", None, "seq")
        return jax.shard_map(
            plain_local if sizes is None else functools.partial(fused_local, sizes),
            mesh=mesh,
            in_specs=(by_token, by_head, by_head, by_head, by_token, by_head, by_head)
            + (P(), P(), rows, rows, rows, rows),
            out_specs=(rows, rows, rows, rows),
            check_vma=False,
        )(*arrays)

    return step
```

```python
import functools
import math

import jax
import jax.numpy as jnp
from jax import lax
from jax.experimental import pallas as pl
from jax.experimental.pallas import tpu as pltpu
from jax.sharding import PartitionSpec as P

HEAD_SIZE = 128
LANES = 128
PAIR = 2
GROUP = 2
MESH = pl.DeviceIdType.MESH


beta_first = 0.9
beta_second = 0.95
learn_rate = 0.02
decay_weight = 0.1
ema_decay = 0.999
adam_epsilon = 1e-08
adapter_factor = 2.0


def for_sending(array):
    return jax.tree.map(lambda a: a.astype(jnp.bfloat16) if a.dtype == jnp.float32 else a, array)


def contract_dims(first_op, second_op, first_dim, second_dim):
    return lax.dot_general(
        first_op,
        second_op,
        (((first_dim,), (second_dim,)), ((), ())),
        preferred_element_type=jnp.float32,
    )


def attend_blocks(query_rows, key_rows, value_rows, grad_rows, delta_row, outside_row):
    factor = query_rows.shape[-1] ** (-0.5)
    length = query_rows.shape[0]
    block_rows = 512
    query_parts = []
    value_total = jnp.zeros(value_rows.shape, jnp.float32)
    for block_index in range(length // block_rows):
        rows = slice(block_index * block_rows, (block_index + 1) * block_rows)
        query_block = query_rows[rows]
        grad_block = grad_rows[rows]
        outside_col = outside_row[rows][:, None]
        score = contract_dims(query_block, key_rows, 1, 1) * factor
        top_score = jnp.maximum(jnp.max(score, axis=1, keepdims=True), outside_col)
        expo = jnp.exp(score - top_score)
        denom = jnp.sum(expo, axis=1, keepdims=True) + jnp.exp(outside_col - top_score)
        probs = expo / denom
        probs_low = probs.astype(jnp.bfloat16)
        value_total = value_total + contract_dims(probs_low, grad_block, 0, 0)
        grad_prob = contract_dims(grad_block, value_rows, 1, 1)
        grad_score = (probs * (grad_prob - delta_row[rows][:, None])).astype(jnp.bfloat16)
        query_parts.append(
            (contract_dims(grad_score, key_rows, 1, 0) * factor).astype(jnp.bfloat16)
        )
    grad_query = jnp.concatenate(query_parts, axis=0)
    grad_value = value_total.astype(jnp.bfloat16)
    return (grad_query, grad_value)


def adapter_terms(input_arrays, gradient_list, adapter_down_factors, adapter_up_factors):
    adapter_width = adapter_up_factors.shape[0] // 2
    projected_rows = jnp.dot(
        input_arrays, adapter_down_factors, preferred_element_type=jnp.float32
    ).astype(jnp.bfloat16)
    middle_rows = jnp.concatenate(
        [
            contract_dims(
                gradient_list[adapter_pair],
                adapter_up_factors[
                    adapter_pair * adapter_width : (adapter_pair + 1) * adapter_width
                ],
                1,
                1,
            )
            for adapter_pair in range(2)
        ],
        axis=1,
    ).astype(jnp.bfloat16)
    down_gradient = adapter_factor * contract_dims(input_arrays, middle_rows, 0, 0)
    up_gradient = jnp.concatenate(
        [
            adapter_factor
            * contract_dims(
                projected_rows[
                    :, adapter_pair * adapter_width : (adapter_pair + 1) * adapter_width
                ],
                gradient_list[adapter_pair],
                0,
                0,
            )
            for adapter_pair in range(2)
        ],
        axis=0,
    )
    return (down_gradient, up_gradient)


def adam_update(grads, float_params, first_moments, second_moments, average_params):
    first_new = beta_first * first_moments + (1.0 - beta_first) * grads
    second_new = beta_second * second_moments + (1.0 - beta_second) * grads * grads
    master_new = float_params - learn_rate * (
        first_new / (jnp.sqrt(second_new) + adam_epsilon) + decay_weight * float_params
    )
    ema_new = ema_decay * average_params + (1.0 - ema_decay) * master_new
    return (master_new, first_new, second_new, ema_new)


def plain_local(
    normed_tokens,
    query_by_head,
    key_by_head,
    value_by_head,
    output_gradient,
    delta_by_head,
    outer_log_mass,
    adapter_down_factors,
    adapter_up_factors,
    float_params,
    first_moments,
    second_moments,
    average_params,
):
    grad_heads = lax.all_to_all(output_gradient, "seq", split_axis=2, concat_axis=1, tiled=True)
    length = query_by_head.shape[1]
    local_count = query_by_head.shape[2] // HEAD_SIZE

    def split_local(array):
        return array[0].reshape(length, local_count, HEAD_SIZE).transpose(1, 0, 2)

    def merge_local(array):
        return array.transpose(1, 0, 2).reshape(length, local_count * HEAD_SIZE)[None]

    bundle_in = (
        split_local(query_by_head),
        split_local(key_by_head),
        split_local(value_by_head),
        split_local(grad_heads),
        delta_by_head[0].T,
        outer_log_mass[0].T,
    )
    query_stack, value_stack = lax.map(lambda bundle: attend_blocks(*bundle), bundle_in)
    local_query = merge_local(query_stack)
    local_value = merge_local(value_stack)
    token_queries, token_values = (
        lax.all_to_all(
            for_sending(local_query), "seq", split_axis=1, concat_axis=2, tiled=True
        ).astype(local_query.dtype),
        lax.all_to_all(
            for_sending(local_value), "seq", split_axis=1, concat_axis=2, tiled=True
        ).astype(local_value.dtype),
    )
    down_gradient, up_gradient = adapter_terms(
        normed_tokens[0],
        [token_queries[0], token_values[0]],
        adapter_down_factors,
        adapter_up_factors,
    )
    term_rows = jnp.concatenate([down_gradient.reshape(-1), up_gradient.reshape(-1)]).reshape(
        -1, 128
    )
    partial_rows = lax.psum_scatter(term_rows, "dp", scatter_dimension=0, tiled=True)
    grads = lax.psum_scatter(partial_rows, "seq", scatter_dimension=0, tiled=True)
    master_new, first_new, second_new, ema_new = adam_update(
        grads, float_params, first_moments, second_moments, average_params
    )
    return (master_new, first_new, second_new, ema_new)


def fused_kernel(
    sizes,
    x_hbm,
    q_hbm,
    k_hbm,
    v_hbm,
    g_hbm,
    delta_hbm,
    mass_hbm,
    down_hbm,
    up_hbm,
    grads_ref,
    x_ref,
    q_ref,
    k_ref,
    v_ref,
    g_ref,
    delta_rows,
    mass_rows,
    down_ref,
    up_ref,
    proj_ref,
    probs_ref,
    gq_ref,
    gv_ref,
    mid_acc,
    mid_send,
    mid_recv,
    up_acc,
    up_send,
    up_recv,
    x_part,
    down_send,
    down_recv,
    flat_ref,
    load_sem,
    ready_sem,
    g_send_sem,
    g_recv_sem,
    x_send_sem,
    x_recv_sem,
    proj_send_sem,
    proj_recv_sem,
    mid_send_sem,
    mid_recv_sem,
    down_send_sem,
    down_recv_sem,
    up_send_sem,
    up_recv_sem,
):
    n_seq, nz = sizes["n_seq"], sizes["nz"]
    places = PAIR * n_seq
    down_count, down_block, up_rows = sizes["down_count"], sizes["down_block"], sizes["up_rows"]
    rank2 = up_ref.shape[0]
    width = q_ref.shape[1]
    heads = width // HEAD_SIZE
    length = q_ref.shape[0]
    tokens = x_ref.shape[0]
    factor = HEAD_SIZE ** (-0.5)

    my_dp, me = lax.axis_index("dp"), lax.axis_index("seq")
    my_z, my_core = my_dp // PAIR, my_dp % PAIR
    my_place = my_core * n_seq + me
    my_flat = my_dp * n_seq + me
    member, first_member = my_dp % GROUP, my_dp // GROUP * GROUP
    teams = nz * PAIR // GROUP
    owners = nz * places
    share = down_count // GROUP
    part = share * down_block

    def plane_device(place):
        return (my_z * PAIR + place // n_seq, place % n_seq)

    def line_device(z):
        return (z * PAIR + my_core, me)

    def flat_device(owner):
        return (owner // n_seq, owner % n_seq)

    barrier = pltpu.get_barrier_semaphore()

    def greet(device):
        pl.semaphore_signal(barrier, inc=1, device_id=device, device_id_type=MESH)

    for step in range(1, places):
        greet(plane_device(lax.rem(my_place + step, places)))
    for step in range(1, nz):
        greet(line_device(lax.rem(my_z + step, nz)))
    greeted = places - 1 + nz - 1
    for step in range(PAIR, GROUP, PAIR):
        for core in range(1, PAIR):
            other = first_member + lax.rem(member // PAIR * PAIR + step, GROUP) + lax.rem(my_core + core, PAIR)
            greet((other, me))
            greeted += 1

    my_columns = pl.ds(pl.multiple_of(me * width, LANES), width)
    my_tokens = pl.ds(pl.multiple_of(me * tokens, LANES), tokens)
    loads = [
        pltpu.make_async_copy(source, target, load_sem.at[index])
        for index, (source, target) in enumerate(
            (
                (mass_hbm, mass_rows),
                (k_hbm.at[0], k_ref),
                (q_hbm.at[0], q_ref),
                (x_hbm.at[0], x_ref),
                (down_hbm, down_ref),
                (delta_hbm, delta_rows),
                (v_hbm.at[0], v_ref),
                (g_hbm.at[0, :, my_columns], g_ref.at[my_tokens, :]),
                (up_hbm.at[:, my_columns], up_ref),
                (
                    x_hbm.at[0, :, pl.ds(pl.multiple_of(member * part, LANES), part)],
                    x_part.at[pl.ds(pl.multiple_of(member * tokens, LANES), tokens), :],
                ),
            )
        )
    ]
    for load in loads:
        load.start()
    def g_copy(step, head):
        target = lax.rem(me + step, n_seq)
        source_columns = pl.ds(pl.multiple_of(target * width + head * HEAD_SIZE, LANES), HEAD_SIZE)
        return pltpu.make_async_remote_copy(
            src_ref=g_hbm.at[0, :, source_columns],
            dst_ref=g_ref.at[my_tokens, pl.ds(pl.multiple_of(head * HEAD_SIZE, LANES), HEAD_SIZE)],
            send_sem=g_send_sem.at[step, head],
            recv_sem=g_recv_sem.at[step, head],
            device_id=(my_dp, target),
            device_id_type=MESH,
        )

    def x_copy(step):
        target = lax.rem(member + step, GROUP)
        return pltpu.make_async_remote_copy(
            src_ref=x_hbm.at[0, :, pl.ds(pl.multiple_of(target * part, LANES), part)],
            dst_ref=x_part.at[pl.ds(pl.multiple_of(member * tokens, LANES), tokens), :],
            send_sem=x_send_sem.at[step],
            recv_sem=x_recv_sem.at[step],
            device_id=(first_member + target, me),
            device_id_type=MESH,
        )

    def proj_copy(step):
        return pltpu.make_async_remote_copy(
            src_ref=proj_ref.at[me],
            dst_ref=proj_ref.at[me],
            send_sem=proj_send_sem.at[step],
            recv_sem=proj_recv_sem.at[step],
            device_id=(my_dp, lax.rem(me + step, n_seq)),
            device_id_type=MESH,
        )

    block = min(256, length)

    def columns_of(head):
        return pl.ds(pl.multiple_of(head * HEAD_SIZE, LANES), HEAD_SIZE)

    def forward(head, carry):
        columns = columns_of(head)
        keys = k_ref[:, columns]
        for start in range(0, length, block):
            score = contract_dims(keys, q_ref[start : start + block, columns], 1, 1) * factor
            outside = mass_rows[head, :, start : start + block]
            top = jnp.maximum(jnp.max(score, axis=0, keepdims=True), outside)
            expo = jnp.exp(score - top)
            denom = jnp.sum(expo, axis=0, keepdims=True) + jnp.exp(outside - top)
            probs_ref[head, :, start : start + block] = (expo * (1.0 / denom)).astype(jnp.bfloat16)
        return carry

    pl.semaphore_wait(barrier, greeted)
    for head in range(heads):
        for step in range(1, n_seq):
            g_copy(step, head).start()
    for step in range(1, GROUP):
        x_copy(step).start()
    for step in range(1, places):
        pl.semaphore_signal(
            ready_sem,
            inc=1,
            device_id=plane_device(lax.rem(my_place + step, places)),
            device_id_type=MESH,
        )

    for load in loads[:3]:
        load.wait()
    lax.fori_loop(0, heads, forward, 0)
    for load in loads[3:]:
        load.wait()
    projected = contract_dims(down_ref[...], x_ref[...], 1, 1)
    proj_ref[me] = projected.astype(jnp.bfloat16).astype(jnp.float32)
    for step in range(1, n_seq):
        proj_copy(step).start()
    mid_acc[...] = jnp.zeros_like(mid_acc)

    def backward(head, carry):
        columns = columns_of(head)
        for step in range(1, n_seq):
            g_copy(step, head).wait_recv()
        keys_turned = jnp.transpose(k_ref[:, columns])
        values = v_ref[:, columns]
        up_head = up_ref[:, columns]
        grad_prob = contract_dims(values, g_ref[:, columns], 1, 1)
        probs = probs_ref[head].astype(jnp.float32)
        grad_score = (probs * (grad_prob - delta_rows[head])).astype(jnp.bfloat16)
        grad_q = (contract_dims(keys_turned, grad_score, 1, 0) * factor).astype(jnp.bfloat16)
        gq_ref[columns, :] = grad_q
        mids_q = contract_dims(up_head, grad_q, 1, 0)
        grad_v = contract_dims(probs_ref[head], g_ref[:, columns], 1, 0).astype(jnp.bfloat16)
        gv_ref[:, columns] = grad_v
        mids_v = contract_dims(up_head, grad_v, 1, 1)
        mid_first = lax.broadcasted_iota(jnp.int32, (rank2, length), 0) < rank2 // 2
        mid_acc[...] += jnp.where(mid_first, mids_q, mids_v)
        return carry

    lax.fori_loop(0, heads, backward, 0)

    for s in range(n_seq):
        mid_send[s] = mid_acc[:, s * tokens : (s + 1) * tokens].astype(mid_send.dtype)
    pl.semaphore_wait(ready_sem, places - 1)

    my_slot = member * n_seq + me
    slots = GROUP * n_seq

    def mid_copy(step):
        target = lax.rem(my_slot + step, slots)
        return pltpu.make_async_remote_copy(
            src_ref=mid_send.at[target % n_seq],
            dst_ref=mid_recv.at[my_slot],
            send_sem=mid_send_sem.at[step],
            recv_sem=mid_recv_sem.at[step],
            device_id=(first_member + target // n_seq, target % n_seq),
            device_id_type=MESH,
        )

    for step in range(1, slots):
        mid_copy(step).start()
    mid_recv[my_slot] = mid_send[me]

    for step in range(1, n_seq):
        proj_copy(step).wait_recv()
    proj_all = jnp.concatenate([proj_ref[s] for s in range(n_seq)], axis=1).astype(jnp.bfloat16)
    up_q = contract_dims(proj_all, gq_ref[...], 1, 1)
    up_v = contract_dims(proj_all, gv_ref[...], 1, 0)
    up_first = lax.broadcasted_iota(jnp.int32, (rank2, width), 0) < rank2 // 2
    up_acc[...] = adapter_factor * jnp.where(up_first, up_q, up_v)

    def up_copy(index):
        return pltpu.make_async_remote_copy(
            src_ref=up_send.at[index],
            dst_ref=up_recv.at[my_dp, me],
            send_sem=up_send_sem.at[index],
            recv_sem=up_recv_sem.at[my_dp, me],
            device_id=flat_device(down_count + index),
            device_id_type=MESH,
        )

    for index in range(owners - down_count):
        piece = up_acc[index * up_rows : (index + 1) * up_rows, :]
        up_send[index] = piece

        @pl.when(down_count + index != my_flat)
        def _():
            up_copy(index).start()

        @pl.when(down_count + index == my_flat)
        def _():
            up_recv[my_dp, me] = piece

    for step in range(1, slots):
        mid_copy(step).wait_recv()
    mids = []
    for m in range(GROUP):
        total = mid_recv[m * n_seq].astype(jnp.float32)
        for s in range(1, n_seq):
            total = total + mid_recv[m * n_seq + s].astype(jnp.float32)
        mids.append(total.astype(jnp.bfloat16))
    mids = jnp.concatenate(mids, axis=1)
    for step in range(1, GROUP):
        x_copy(step).wait_recv()

    my_source = my_dp // GROUP * n_seq + me

    def down_copy(index):
        return pltpu.make_async_remote_copy(
            src_ref=down_send.at[index],
            dst_ref=down_recv.at[my_source],
            send_sem=down_send_sem.at[index],
            recv_sem=down_recv_sem.at[my_source],
            device_id=flat_device(member * share + index),
            device_id_type=MESH,
        )

    for index in range(share):
        piece = contract_dims(mids, x_part[:, index * down_block : (index + 1) * down_block], 1, 0)
        piece = (adapter_factor * piece).astype(down_send.dtype)
        down_send[index] = piece

        @pl.when(member * share + index != my_flat)
        def _():
            down_copy(index).start()

        @pl.when(member * share + index == my_flat)
        def _():
            down_recv[my_source] = piece

    def arrived(buffer, semaphore):
        pltpu.make_async_remote_copy(
            src_ref=buffer,
            dst_ref=buffer,
            send_sem=semaphore,
            recv_sem=semaphore,
            device_id=plane_device(lax.rem(my_place + 1, places)),
            device_id_type=MESH,
        ).wait_recv()

    own_down = my_flat < down_count

    @pl.when(own_down)
    def _():
        from_me = my_flat // share == member
        for source in range(teams * n_seq):

            @pl.when(jnp.logical_not(from_me & (my_source == source)))
            def _():
                arrived(down_recv.at[source], down_recv_sem.at[source])

        total = down_recv[0].astype(jnp.float32)
        for source in range(1, teams * n_seq):
            total = total + down_recv[source].astype(jnp.float32)
        padding = jnp.zeros((LANES - rank2, down_block), jnp.float32)
        flat_ref[...] = jnp.transpose(jnp.concatenate([total, padding], axis=0))
        period = LANES // math.gcd(LANES, rank2)
        span = period * rank2 // LANES
        groups = down_block // period
        lane = lax.broadcasted_iota(jnp.int32, (groups, LANES), 1)
        out_rows = [jnp.zeros((groups, LANES), jnp.float32) for _ in range(span)]
        for index in range(period):
            row, offset = divmod(index * rank2, LANES)
            entry = flat_ref[pl.ds(index, groups, stride=period), :]
            if offset:
                entry = pltpu.roll(entry, offset, 1)
            if offset + rank2 > LANES:
                out_rows[row] = out_rows[row] + jnp.where(lane >= offset, entry, 0.0)
                out_rows[row + 1] = out_rows[row + 1] + jnp.where(lane < offset, entry, 0.0)
            else:
                out_rows[row] = out_rows[row] + entry
        for row in range(span):
            grads_ref[pl.ds(row, groups, stride=span), :] = out_rows[row]

    @pl.when(jnp.logical_not(own_down))
    def _():
        for dp in range(nz * PAIR):
            for s in range(n_seq):

                @pl.when(dp * n_seq + s != my_flat)
                def _():
                    arrived(up_recv.at[dp, s], up_recv_sem.at[dp, s])

        for s in range(n_seq):
            total = up_recv[0, s]
            for dp in range(1, nz * PAIR):
                total = total + up_recv[dp, s]
            for row in range(up_rows):
                for tile in range(heads):
                    target = (row * n_seq + s) * heads + tile
                    grads_ref[target : target + 1, :] = total[
                        row : row + 1, tile * HEAD_SIZE : (tile + 1) * HEAD_SIZE
                    ]

    for step in range(1, n_seq):
        for head in range(heads):
            g_copy(step, head).wait_send()
        proj_copy(step).wait_send()
    for step in range(1, GROUP):
        x_copy(step).wait_send()
    for step in range(1, slots):
        mid_copy(step).wait_send()
    for index in range(owners - down_count):

        @pl.when(down_count + index != my_flat)
        def _():
            up_copy(index).wait_send()

    for index in range(share):

        @pl.when(member * share + index != my_flat)
        def _():
            down_copy(index).wait_send()


def fused_local(sizes, *arrays):
    (tokens_in, query, key, value, out_grad, delta, mass, down, up) = arrays[:9]
    n_seq, nz = sizes["n_seq"], sizes["nz"]
    places = PAIR * n_seq
    down_count, down_block, up_rows = sizes["down_count"], sizes["down_block"], sizes["up_rows"]
    up_count = nz * places - down_count
    tokens, model = tokens_in.shape[1:]
    length, width = query.shape[1:]
    heads = width // HEAD_SIZE
    rank2 = up.shape[0]
    teams, slots = nz * PAIR // GROUP, GROUP * n_seq
    share = down_count // GROUP
    f32, bf16 = jnp.float32, jnp.bfloat16
    dma = pltpu.SemaphoreType.DMA
    grads = pl.pallas_call(
        functools.partial(fused_kernel, sizes),
        out_shape=jax.ShapeDtypeStruct(arrays[9].shape, f32),
        in_specs=[pl.BlockSpec(memory_space=pl.ANY)] * 9,
        out_specs=pl.BlockSpec(memory_space=pltpu.VMEM),
        scratch_shapes=[
            pltpu.VMEM((tokens, model), bf16),
            pltpu.VMEM((length, width), bf16),
            pltpu.VMEM((length, width), bf16),
            pltpu.VMEM((length, width), bf16),
            pltpu.VMEM((length, width), bf16),
            pltpu.VMEM((heads, 1, length), f32),
            pltpu.VMEM((heads, 1, length), f32),
            pltpu.VMEM((rank2, model), bf16),
            pltpu.VMEM((rank2, width), bf16),
            pltpu.VMEM((n_seq, rank2, tokens), f32),
            pltpu.VMEM((heads, length, length), bf16),
            pltpu.VMEM((width, length), bf16),
            pltpu.VMEM((length, width), bf16),
            pltpu.VMEM((rank2, length), f32),
            pltpu.VMEM((n_seq, rank2, tokens), bf16),
            pltpu.VMEM((slots, rank2, tokens), bf16),
            pltpu.VMEM((rank2, width), f32),
            pltpu.VMEM((up_count, up_rows, width), f32),
            pltpu.VMEM((nz * PAIR, n_seq, up_rows, width), f32),
            pltpu.VMEM((GROUP * tokens, share * down_block), bf16),
            pltpu.VMEM((share, rank2, down_block), bf16),
            pltpu.VMEM((teams * n_seq, rank2, down_block), bf16),
            pltpu.VMEM((down_block, LANES), f32),
            dma((10,)),
            pltpu.SemaphoreType.REGULAR,
            dma((n_seq, heads)),
            dma((n_seq, heads)),
            dma((GROUP,)),
            dma((GROUP,)),
            dma((n_seq,)),
            dma((n_seq,)),
            dma((slots,)),
            dma((slots,)),
            dma((share,)),
            dma((teams * n_seq,)),
            dma((up_count,)),
            dma((nz * PAIR, n_seq)),
        ],
        compiler_params=pltpu.CompilerParams(
            collective_id=0, has_side_effects=True, vmem_limit_bytes=24 * 1024 * 1024
        ),
        name="fused",
    )(
        *[
            pltpu.with_memory_space_constraint(array, pltpu.HBM)
            for array in (tokens_in, query, key, value, out_grad)
            + (delta.transpose(2, 0, 1), mass.transpose(2, 0, 1), down.T, up)
        ]
    )
    return adam_update(grads, *arrays[9:])


def fused_sizes(mesh, shapes):
    n_dp, n_seq = mesh.shape["dp"], mesh.shape["seq"]
    down, up, rows = shapes
    count = rows[0] // (n_dp * n_seq) * rows[1]
    if n_dp % PAIR or n_dp % GROUP or count % down[1] or count % up[1]:
        return None
    block, up_rows = count // down[1], count // up[1]
    period = LANES // math.gcd(LANES, down[1])
    if down[0] % (block * GROUP) or block % LANES or block % period or up[0] % up_rows:
        return None
    return {
        "n_seq": n_seq,
        "nz": n_dp // PAIR,
        "down_count": down[0] // block,
        "down_block": block,
        "up_rows": up_rows,
    }


def solution(mesh):
    def step(*arrays):
        sizes = fused_sizes(mesh, (arrays[7].shape, arrays[8].shape, arrays[9].shape))
        rows = P(("dp", "seq"), None)
        by_token, by_head = P("dp", "seq", None), P("dp", None, "seq")
        return jax.shard_map(
            plain_local if sizes is None else functools.partial(fused_local, sizes),
            mesh=mesh,
            in_specs=(by_token, by_head, by_head, by_head, by_token, by_head, by_head)
            + (P(), P(), rows, rows, rows, rows),
            out_specs=(rows, rows, rows, rows),
            check_vma=False,
        )(*arrays)

    return step
```
